256 devices in a mesh: ctx: 32 (over x_lo, z, core), head: 8 (over x_hi, y).
Axes of the slice: x: 4 (x_hi: 2, x_lo: 2; x = x_hi * 2 + x_lo), y: 4, z: 8, core: 2. Of those that a mesh axis runs over, the one named last changes fastest.
Arguments:
- tokens: bfloat16 [8192, 3072], P('ctx', 'head'), may hold values from -48 to 48
- block_order: int32 [64], replicated, may hold values from 0 to 63, each once
- block_mask: int32 [64, 64], replicated, may hold values from 0 to 1, as said below
- w_query: bfloat16 [3072, 3072], P(None, 'head'), may hold values from -0.109375 to 0.109375
- w_key: bfloat16 [3072, 3072], P(None, 'head'), may hold values from -0.109375 to 0.109375
- w_value: bfloat16 [3072, 3072], P(None, 'head'), may hold values from -0.109375 to 0.109375
- w_out: bfloat16 [3072, 3072], P('head'), may hold values from -0.109375 to 0.109375
Outputs:
- mixed: bfloat16 [8192, 3072], P('ctx', 'head')
The draws below stay inside these ranges and needn't reach their ends.
Inputs may be any that keep to these rules, and one draw needn't show every extreme that they name: `block_order`: a permutation of the block numbers. block_mask[f, f] = 1 for every block f.
All inputs are finite; a program needn't handle non-finite values.
Results may differ from the reference program's by a relative error of at most 0.02.
The reference program's roundings to bfloat16 on the way count: a program that leaves them out, or rounds other values in their place, can miss the bound.
Values may be sent and summed in bfloat16 or wider, within the bound.
A program may use at most 128 MiB of HBM per device.

```python
import jax
import jax.numpy as jnp
from jax import lax

D = 3072
HEADS = 24
HEAD_DIM = 128
BLOCK = 128
FRAME_BLOCKS = 8
TOKENS = 8192
NB = 64
N_HEAD = 8


def draw_tokens(key, part):
    return jnp.clip(jax.random.normal(key, (TOKENS, D), jnp.float32), -6.0, 6.0).astype(jnp.bfloat16)


def draw_block_mask(key, part):
    places = jnp.arange(NB, dtype=jnp.int32)
    frame_index = places // FRAME_BLOCKS
    spot_index = places % FRAME_BLOCKS
    distance = jnp.abs(frame_index[:, None] - frame_index[None, :])
    level = jnp.zeros((NB, NB), jnp.int32)
    for power in range(16):
        level = level + (distance >= 2 ** power).astype(jnp.int32)
    band_width = jnp.maximum(jnp.right_shift(jnp.int32(FRAME_BLOCKS), level), 1)
    radial = jnp.abs(spot_index[:, None] - spot_index[None, :]) < band_width
    extra = jax.random.randint(key, (NB, NB), 0, 8) == 0
    diagonal = places[:, None] == places[None, :]
    return (radial | extra | diagonal).astype(jnp.int32)


def steps_of(own_key, dims, shards, least, high):
    factor_of = 1.0
    for dim, shards_of in shards:
        draws = jax.random.uniform(jax.random.fold_in(jax.random.fold_in(own_key, 6), dim), (shards_of,), jnp.float32, least / len(shards), high / len(shards))
        factor_of = factor_of * jnp.repeat(jnp.exp(draws), dims[dim] // shards_of).reshape((-1,) + (1,) * (len(dims) - 1 - dim))
    return factor_of


def normal_values(own_key, extent, scale, most, cuts=(), kind=jnp.bfloat16):
    result = scale * jax.random.normal(own_key, extent, jnp.float32)
    if cuts:
        result = result * steps_of(own_key, extent, cuts, -0.22, 0.18)
    return jnp.clip(result, -most, most).astype(kind)


def setup_inputs(seed: int = 0) -> dict:
    arg_keys = jax.random.split(jax.random.key(seed), 8)
    tokens = draw_tokens(jax.random.fold_in(arg_keys[7], 71), 0)
    block_order = jax.random.permutation(arg_keys[1], NB).astype(jnp.int32)
    block_mask = draw_block_mask(jax.random.fold_in(arg_keys[7], 71), 0)
    w_query = normal_values(arg_keys[3], (D, D), D ** -0.5, 0.109375, ((1, 8),))
    w_key = normal_values(arg_keys[4], (D, D), D ** -0.5, 0.109375, ((1, 8),))
    w_value = normal_values(arg_keys[5], (D, D), D ** -0.5, 0.109375, ((1, 8),))
    w_out = normal_values(arg_keys[6], (D, D), D ** -0.5, 0.109375, ((0, 8),))
    return {"tokens": tokens, "block_order": block_order, "block_mask": block_mask, "w_query": w_query, "w_key": w_key, "w_value": w_value, "w_out": w_out}


def reference(tokens, block_order, block_mask, w_query, w_key, w_value, w_out):
    query_rows = jnp.dot(tokens, w_query, preferred_element_type=jnp.float32).astype(jnp.bfloat16)
    key_rows = jnp.dot(tokens, w_key, preferred_element_type=jnp.float32).astype(jnp.bfloat16)
    value_rows = jnp.dot(tokens, w_value, preferred_element_type=jnp.float32).astype(jnp.bfloat16)
    query_tiles = query_rows.astype(jnp.float32).reshape(TOKENS // BLOCK, BLOCK, HEADS, HEAD_DIM)
    key_all = key_rows.astype(jnp.float32).reshape(TOKENS, HEADS, HEAD_DIM)
    value_all = value_rows.astype(jnp.float32).reshape(TOKENS, HEADS, HEAD_DIM)
    cycle_live = block_mask[block_order][:, block_order]
    inv_root = 1.0 / (HEAD_DIM ** 0.5)

    def one_block(inputs):
        query_tile, live_row = inputs
        key_keep = jnp.repeat(live_row, BLOCK) > 0
        scores = jnp.einsum("qhd,khd->hqk", query_tile, key_all) * inv_root
        allowed = key_keep[None, None, :]
        row_top = jnp.max(jnp.where(allowed, scores, -1e30), axis=-1)
        weights = jnp.where(allowed, jnp.exp(scores - row_top[..., None]), 0.0)
        row_total = jnp.sum(weights, axis=-1)
        rounded = weights.astype(jnp.bfloat16).astype(jnp.float32)
        attended_tile = jnp.einsum("hqk,khd->hqd", rounded, value_all) / row_total[..., None]
        return attended_tile.transpose(1, 0, 2).reshape(BLOCK, D).astype(jnp.bfloat16)

    attended = lax.map(one_block, (query_tiles, cycle_live)).reshape(TOKENS, D)
    group_width = D // N_HEAD
    mixed_sum = jnp.zeros((TOKENS, D), jnp.float32)
    for group in range(N_HEAD):
        group_part = jnp.dot(attended[:, group * group_width:(group + 1) * group_width],
                             w_out[group * group_width:(group + 1) * group_width],
                             preferred_element_type=jnp.float32).astype(jnp.bfloat16)
        mixed_sum = mixed_sum + group_part.astype(jnp.float32)
    return mixed_sum.astype(jnp.bfloat16)
```

```python
import functools

import jax
import jax.numpy as jnp
from jax import lax
from jax.experimental import pallas as pl
from jax.experimental.pallas import tpu as pltpu
from jax.sharding import PartitionSpec as P

MESH = pl.DeviceIdType.MESH
HD = 128
BLK = 128
HEADS = 3
ROWS = 256
COLS = 384
NX, NY, NZ = 4, 4, 8
UNITS = 2 * HEADS
DEPTH = 3
NEG = -1e30
SCALE2 = 1.4426950408889634 / HD**0.5


def kernel(
    order_ref, mask_ref, tok_in, wq_hbm, wk_hbm, wv_hbm, wo_hbm, out_ref,
    tok, wbuf, wo, acc, qall, kv, m_s, l_s, o_s, osend, ssend, orecv, srecv, asend, att, out_acc,
    w_sem, xs, xr, ys, yr, zs, zr, qs, qr, os_, or_, ss_, sr_, axs, axr, ays, ayr, ws, wr, ps, pr,
):
    ctx = lax.axis_index("ctx")
    hd = lax.axis_index("head")
    x_lo, z, c = ctx // 16, (ctx // 2) % 8, ctx % 2
    x_hi, y = hd // 4, hd % 4
    x = 2 * x_hi + x_lo

    def dev(xx, yy, zz, cc):
        return ((xx % 2) * 16 + zz * 2 + cc, (xx // 2) * 4 + yy)

    xp, xm = (x + 1) % NX, (x + NX - 1) % NX
    yp, ym, y2 = (y + 1) % NY, (y + NY - 1) % NY, (y + 2) % NY
    zp, zm = (z + 1) % NZ, (z + NZ - 1) % NZ
    xn = x_hi * 2 + (1 - x_lo)
    xc = NX - 1 - x
    pc = 1 - c
    d_xp, d_xm = dev(xp, y, z, c), dev(xm, y, z, c)
    d_yp, d_ym = dev(x, yp, z, c), dev(x, ym, z, c)
    d_zp, d_zm = dev(x, y, zp, c), dev(x, y, zm, c)
    sibs = (dev(x, y, z, pc), dev(xn, y, z, c), dev(xn, y, z, pc))
    sib_slot = (x_lo * 2 + pc, (1 - x_lo) * 2 + c, (1 - x_lo) * 2 + pc)
    me_slot = x_lo * 2 + c
    wpeers = [
        (x_hi * 4 + yp, dev(x, yp, z, c), 0), (x_hi * 4 + ym, dev(x, ym, z, c), 1),
        (x_hi * 4 + y2, dev(x, y2, z, c), 2), ((1 - x_hi) * 4 + y, dev(xc, y, z, c), 3),
        ((1 - x_hi) * 4 + yp, dev(xc, yp, z, c), 4), ((1 - x_hi) * 4 + ym, dev(xc, ym, z, c), 5),
        ((1 - x_hi) * 4 + y2, dev(xc, y2, z, c), 6),
    ]
    back = (1, 0, 2, 3, 5, 4, 6)

    started = []

    def send(src, dst, s_sem, r_sem, to):
        copy = pltpu.make_async_remote_copy(
            src_ref=src, dst_ref=dst, send_sem=s_sem, recv_sem=r_sem,
            device_id=to, device_id_type=MESH,
        )
        copy.start()
        started.append(copy)

    def arrived(ref, s_sem, r_sem):
        pltpu.make_async_remote_copy(
            src_ref=ref, dst_ref=ref, send_sem=s_sem, recv_sem=r_sem,
            device_id=d_zp, device_id_type=MESH,
        ).wait_recv()

    loads = [
        pltpu.make_async_copy(w, wbuf.at[i], w_sem.at[i])
        for i, w in enumerate((wk_hbm, wv_hbm, wq_hbm))
    ]
    for load in loads:
        load.start()
    own_out = pltpu.make_async_copy(
        wo_hbm.at[:, pl.ds(pl.multiple_of(hd * COLS, COLS), COLS)], wo.at[hd], w_sem.at[3]
    )
    own_out.start()

    barrier = pltpu.get_barrier_semaphore()
    peers = [d_xp, d_xm, d_yp, d_ym, d_zp, d_zm, sibs[0], sibs[2]]
    peers += [wpeers[2][1], wpeers[4][1], wpeers[5][1], wpeers[6][1]]
    for peer in peers:
        pl.semaphore_signal(barrier, inc=1, device_id=peer, device_id_type=MESH)
    pl.semaphore_wait(barrier, len(peers))

    send(tok_in, tok.at[hd], xs.at[0], xr.at[0], d_xp)
    send(tok_in, tok.at[hd], xs.at[1], xr.at[1], d_xm)

    def x_arrived(buf, r_sem, s_sem):
        arrived(buf.at[(xm // 2) * 4 + y], s_sem.at[0], r_sem.at[0])
        arrived(buf.at[(xp // 2) * 4 + y], s_sem.at[1], r_sem.at[1])

    def y_first(buf, s_sem, r_sem):
        send(buf.at[y], buf.at[y], s_sem.at[0], r_sem.at[0], d_yp)
        send(buf.at[4 + y], buf.at[4 + y], s_sem.at[1], r_sem.at[1], d_ym)
        send(buf.at[4 + y], buf.at[4 + y], s_sem.at[2], r_sem.at[2], d_yp)
        send(buf.at[y], buf.at[y], s_sem.at[3], r_sem.at[3], d_ym)

    def y_second(buf, s_sem, r_sem):
        arrived(buf.at[ym], s_sem.at[0], r_sem.at[0])
        send(buf.at[ym], buf.at[ym], s_sem.at[4], r_sem.at[4], d_yp)
        arrived(buf.at[4 + yp], s_sem.at[1], r_sem.at[1])
        send(buf.at[4 + yp], buf.at[4 + yp], s_sem.at[5], r_sem.at[5], d_ym)
        arrived(buf.at[4 + ym], s_sem.at[2], r_sem.at[2])
        arrived(buf.at[yp], s_sem.at[3], r_sem.at[3])

    def y_last(buf, s_sem, r_sem):
        arrived(buf.at[y2], s_sem.at[4], r_sem.at[4])
        arrived(buf.at[4 + y2], s_sem.at[5], r_sem.at[5])

    def project(yy, first):
        for shard in range(2):
            g = shard * 4 + yy

            def one(w, carry, g=g, init=first and shard == 0):
                part = jnp.dot(
                    tok[g], wbuf[w, pl.ds(pl.multiple_of(g * COLS, COLS), COLS), :],
                    preferred_element_type=jnp.float32,
                )
                if init:
                    acc[w] = part
                else:
                    acc[w] = acc[w] + part
                return carry

            lax.fori_loop(0, 3, one, 0)

    x_arrived(tok, xr, xs)
    y_first(tok, ys, yr)
    for load in loads:
        load.wait()
    project(y, True)
    y_second(tok, ys, yr)
    project(ym, False)
    project(yp, False)
    y_last(tok, ys, yr)
    project(y2, False)

    for h in range(HEADS):
        cols = slice(h * HD, (h + 1) * HD)
        kv[z, h, :, 0:HD] = acc[0, :, cols].astype(jnp.bfloat16)
        kv[z, h, :, HD : 2 * HD] = acc[1, :, cols].astype(jnp.bfloat16)
        qall[me_slot, h] = acc[2, :, cols].astype(jnp.bfloat16)

    def piece(zz, u):
        return kv.at[zz, u // 2, pl.ds((u % 2) * BLK, BLK), :]

    def z_send(direction, s, u):
        if s == 4 and direction != u % 2:
            return
        if direction == 0:
            ref, to = piece((z + NZ - (s - 1)) % NZ, u), d_zp
        else:
            ref, to = piece((z + (s - 1)) % NZ, u), d_zm
        send(ref, ref, zs.at[direction, s - 1, u], zr.at[direction, s - 1, u], to)

    def z_arrived(direction, s, u):
        if s == 4 and direction != u % 2:
            return
        src = (z + NZ - s) % NZ if direction == 0 else (z + s) % NZ
        arrived(piece(src, u), zs.at[direction, s - 1, u], zr.at[direction, s - 1, u])

    for u in range(DEPTH):
        z_send(0, 1, u)
        z_send(1, 1, u)
    for i in (1, 2, 0):
        send(qall.at[me_slot], qall.at[me_slot], qs.at[i], qr.at[i], sibs[i])
    half = COLS // 2
    my_half = pl.ds(pl.multiple_of(c * half, half), half)
    other_half = pl.ds(pl.multiple_of(pc * half, half), half)
    for g, to, i in wpeers:
        send(
            wo_hbm.at[my_half, pl.ds(pl.multiple_of(g * COLS, COLS), COLS)],
            wo.at[hd, my_half, :], ws.at[i], wr.at[i], to,
        )

    def relay_out_weights():
        for g, _, i in wpeers:
            arrived(wo.at[g, my_half, :], ws.at[back[i]], wr.at[back[i]])
            send(wo.at[g, my_half, :], wo.at[g, my_half, :], ps.at[i], pr.at[i], sibs[0])

    def out_weights_arrived():
        own_out.wait()
        for g, _, i in wpeers:
            arrived(wo.at[g, other_half, :], ps.at[i], pr.at[i])

    def bias_of(q_slot, qi, src, r):
        q_ctx = (1 - q_slot // 2) * 16 + z * 2 + q_slot % 2
        k_ctx = (1 - x_lo) * 16 + src * 2 + c
        live = mask_ref[order_ref[2 * q_ctx + qi], order_ref[2 * k_ctx + r]]
        return jnp.where(live > 0, 0.0, NEG).astype(jnp.float32)

    def attend(h, s):
        if s == 0:
            srcs = [z]
        elif s == 4:
            srcs = [(z + 4) % NZ]
        else:
            srcs = [(z + NZ - s) % NZ, (z + s) % NZ]

        def body(slot, carry):
            q = qall[slot, h]
            scores = []
            for src in srcs:
                raw = lax.dot_general(
                    q, kv[src, h, :, 0:HD], (((1,), (1,)), ((), ())),
                    preferred_element_type=jnp.float32,
                )
                for r in range(2):
                    block = raw[:, r * BLK : (r + 1) * BLK]
                    scores.append(
                        jnp.concatenate(
                            [
                                block[qi * BLK : (qi + 1) * BLK] * SCALE2 + bias_of(slot, qi, src, r)
                                for qi in range(2)
                            ],
                            axis=0,
                        )
                    )
            top = functools.reduce(jnp.maximum, scores)
            top = jnp.broadcast_to(jnp.max(top, axis=1, keepdims=True), (ROWS, HD))
            if s > 0:
                before = m_s[h, slot]
                top = jnp.maximum(before, top)
                factor = jnp.exp2(before - top)
            weights = [jnp.exp2(score - top) for score in scores]
            total = functools.reduce(jnp.add, weights)
            mixed = None
            for i, src in enumerate(srcs):
                rounded = jnp.concatenate(
                    [weights[2 * i].astype(jnp.bfloat16), weights[2 * i + 1].astype(jnp.bfloat16)],
                    axis=1,
                )
                part = jnp.dot(
                    rounded, kv[src, h, :, HD : 2 * HD], preferred_element_type=jnp.float32
                )
                mixed = part if mixed is None else mixed + part
            if s > 0:
                total = total + l_s[h, slot] * factor
                mixed = mixed + o_s[h, slot] * factor
            m_s[h, slot] = top
            l_s[h, slot] = total
            o_s[h, slot] = mixed
            return carry

        lax.fori_loop(0, 4, body, 0)

    def share(h):
        for i in range(3):
            slot = sib_slot[i]
            osend[h, i] = o_s[h, slot].astype(jnp.bfloat16)
            total = jnp.broadcast_to(
                jnp.sum(l_s[h, slot], axis=1, keepdims=True), (ROWS, HD)
            )
            ssend[h, i, 0:8, :] = jnp.transpose(m_s[h, slot])[0:8]
            ssend[h, i, 8:16, :] = jnp.transpose(total)[0:8]
        for i in (1, 2, 0):
            send(ssend.at[h, i], srecv.at[h, i], ss_.at[h, i], sr_.at[h, i], sibs[i])
            send(osend.at[h, i], orecv.at[h, i], os_.at[h, i], or_.at[h, i], sibs[i])

    def combine(h):
        tops = [m_s[h, me_slot]]
        totals = [
            jnp.broadcast_to(jnp.sum(l_s[h, me_slot], axis=1, keepdims=True), (ROWS, HD))
        ]
        parts = [o_s[h, me_slot]]
        for i in range(3):
            arrived(srecv.at[h, i], ss_.at[h, i], sr_.at[h, i])
            arrived(orecv.at[h, i], os_.at[h, i], or_.at[h, i])
            tops.append(jnp.transpose(jnp.broadcast_to(srecv[h, i, 0:1, :], (HD, ROWS))))
            totals.append(jnp.transpose(jnp.broadcast_to(srecv[h, i, 8:9, :], (HD, ROWS))))
            parts.append(orecv[h, i].astype(jnp.float32))
        top = functools.reduce(jnp.maximum, tops)
        scale = [jnp.exp2(t - top) for t in tops]
        total = functools.reduce(jnp.add, [a * b for a, b in zip(scale, totals)])
        mixed = functools.reduce(jnp.add, [a * b for a, b in zip(scale, parts)])
        asend[h] = (mixed / total).astype(jnp.bfloat16)
        send(asend.at[h], att.at[h, hd], axs.at[h, 0], axr.at[h, 0], d_xp)
        send(asend.at[h], att.at[h, hd], axs.at[h, 1], axr.at[h, 1], d_xm)

    def out_part(h, yy, first):
        for hi in range(2):
            g = hi * 4 + yy
            part = jnp.dot(
                att[h, g], wo[g, h * HD : (h + 1) * HD, :], preferred_element_type=jnp.float32
            )
            if first and hi == 0:
                out_acc[...] = part
            else:
                out_acc[...] = out_acc[...] + part

    def att_first(h):
        x_arrived(att.at[h], axr.at[h], axs.at[h])
        y_first(att.at[h], ays.at[h], ayr.at[h])

    def att_second(h):
        y_second(att.at[h], ays.at[h], ayr.at[h])

    def att_last(h):
        if h == 0:
            out_weights_arrived()
        out_part(h, y, h == 0)
        out_part(h, ym, False)
        out_part(h, yp, False)
        y_last(att.at[h], ays.at[h], ayr.at[h])
        out_part(h, y2, False)

    for k in range(0, UNITS + 4 + 5):
        for s in (4, 3, 2, 1):
            u = k - s
            if 0 <= u < UNITS:
                for direction in range(2):
                    z_arrived(direction, s, u)
                    if s < 4:
                        z_send(direction, s + 1, u)
        if DEPTH <= k + DEPTH < UNITS:
            z_send(0, 1, k + DEPTH)
            z_send(1, 1, k + DEPTH)
        if k == 5:
            relay_out_weights()
        for h in range(HEADS):
            done = 2 * h + 5
            if k == done + 1:
                combine(h)
            if k == done + 2:
                att_first(h)
            if k == done + 3:
                att_second(h)
            if k == done + 4:
                att_last(h)
        if k == 1:
            for i in range(3):
                arrived(qall.at[sib_slot[i]], qs.at[i], qr.at[i])
        for h in range(HEADS):
            s = k - (2 * h + 1)
            if 0 <= s <= 4:
                attend(h, s)
                if s == 4:
                    share(h)

    out_ref[...] = out_acc[...].astype(jnp.bfloat16)
    for copy in started:
        copy.wait_send()


def per_device(tokens, block_order, block_mask, w_query, w_key, w_value, w_out):
    bf, f32 = jnp.bfloat16, jnp.float32
    sem = pltpu.SemaphoreType.DMA
    smem = pl.BlockSpec(memory_space=pltpu.SMEM)
    vmem = pl.BlockSpec(memory_space=pltpu.VMEM)
    anywhere = pl.BlockSpec(memory_space=pl.ANY)
    return pl.pallas_call(
        kernel,
        out_shape=jax.ShapeDtypeStruct((ROWS, COLS), bf),
        in_specs=[smem, smem, vmem, anywhere, anywhere, anywhere, anywhere],
        out_specs=vmem,
        scratch_shapes=[
            pltpu.VMEM((8, ROWS, COLS), bf),
            pltpu.VMEM((3, 3072, COLS), bf),
            pltpu.VMEM((8, COLS, COLS), bf),
            pltpu.VMEM((3, ROWS, COLS), f32),
            pltpu.VMEM((4, HEADS, ROWS, HD), bf),
            pltpu.VMEM((NZ, HEADS, ROWS, 2 * HD), bf),
            pltpu.VMEM((HEADS, 4, ROWS, HD), f32),
            pltpu.VMEM((HEADS, 4, ROWS, HD), f32),
            pltpu.VMEM((HEADS, 4, ROWS, HD), f32),
            pltpu.VMEM((HEADS, 3, ROWS, HD), bf),
            pltpu.VMEM((HEADS, 3, 16, ROWS), f32),
            pltpu.VMEM((HEADS, 3, ROWS, HD), bf),
            pltpu.VMEM((HEADS, 3, 16, ROWS), f32),
            pltpu.VMEM((HEADS, ROWS, HD), bf),
            pltpu.VMEM((HEADS, 8, ROWS, HD), bf),
            pltpu.VMEM((ROWS, COLS), f32),
            sem((4,)),
            sem((2,)), sem((2,)),
            sem((6,)), sem((6,)),
            sem((2, 4, UNITS)), sem((2, 4, UNITS)),
            sem((3,)), sem((3,)),
            sem((HEADS, 3)), sem((HEADS, 3)),
            sem((HEADS, 3)), sem((HEADS, 3)),
            sem((HEADS, 2)), sem((HEADS, 2)),
            sem((HEADS, 6)), sem((HEADS, 6)),
            sem((7,)), sem((7,)),
            sem((7,)), sem((7,)),
        ],
        compiler_params=pltpu.CompilerParams(
            collective_id=0, has_side_effects=True, vmem_limit_bytes=60 * 1024 * 1024
        ),
    )(block_order, block_mask, tokens, w_query, w_key, w_value, w_out)


def solution(mesh):
    in_specs = (
        P("ctx", "head"),
        P(),
        P(),
        P(None, "head"),
        P(None, "head"),
        P(None, "head"),
        P("head", None),
    )
    return jax.shard_map(
        per_device, mesh=mesh, in_specs=in_specs, out_specs=P("ctx", "head"), check_vma=False
    )
```

```python
import functools

import jax
import jax.numpy as jnp
from jax import lax
from jax.experimental import pallas as pl
from jax.experimental.pallas import tpu as pltpu
from jax.sharding import PartitionSpec as P

MESH = pl.DeviceIdType.MESH
HD = 128
BLK = 128
HEADS = 3
ROWS = 256
HALF = 128
COLS = 384
NX, NY, NZ = 4, 4, 8
NEG = -1e30
LOW = -1e20
SCALE2 = 1.4426950408889634 / HD**0.5


START = ((0, 0, 0), (2, 3, 4))
GROUPS = (((0, 1), (1, 1), (1, -1), (2, 1)), ((2, -1), (3, 1), (3, -1), (4, 1)))


def kernel(
    order_ref, mask_ref, tok_in, wq_hbm, wk_hbm, wv_hbm, wo_hbm, out_ref,
    tok, wbuf, wo, acc, qall, kv, m_s, l_s, o_s, o1, s1, o1r, s1r, o2, s2, o2r, s2r, asend, att, out_acc,
    w_sem, xs, xr, ys, yr, zs, zr, qs, qr, cs, cr, as_, axr, ayr, ws, wr,
):
    ctx = lax.axis_index("ctx")
    hd = lax.axis_index("head")
    x_lo, z, c = ctx // 16, (ctx // 2) % 8, ctx % 2
    x_hi, y = hd // 4, hd % 4
    x = 2 * x_hi + x_lo

    def dev(xx, yy, zz, cc):
        return ((xx % 2) * 16 + zz * 2 + cc, (xx // 2) * 4 + yy)

    xp, xm = (x + 1) % NX, (x + NX - 1) % NX
    yp, ym, y2 = (y + 1) % NY, (y + NY - 1) % NY, (y + 2) % NY
    zp, zm = (z + 1) % NZ, (z + NZ - 1) % NZ
    x_far = 1 - x_lo
    xc = NX - 1 - x
    pc = 1 - c
    d_xp, d_xm = dev(xp, y, z, c), dev(xm, y, z, c)
    d_yp, d_ym = dev(x, yp, z, c), dev(x, ym, z, c)
    d_zp, d_zm = dev(x, y, zp, c), dev(x, y, zm, c)
    d_core = dev(x, y, z, pc)
    d_far = dev(x_hi * 2 + x_far, y, z, c)
    wpeers = [
        (x_hi * 4 + yp, dev(x, yp, z, c)), (x_hi * 4 + ym, dev(x, ym, z, c)),
        (x_hi * 4 + y2, dev(x, y2, z, c)), ((1 - x_hi) * 4 + y, dev(xc, y, z, c)),
        ((1 - x_hi) * 4 + yp, dev(xc, yp, z, c)), ((1 - x_hi) * 4 + ym, dev(xc, ym, z, c)),
        ((1 - x_hi) * 4 + y2, dev(xc, y2, z, c)),
    ]

    def send(src, dst, s_sem, r_sem, to):
        pltpu.make_async_remote_copy(
            src_ref=src, dst_ref=dst, send_sem=s_sem, recv_sem=r_sem,
            device_id=to, device_id_type=MESH,
        ).start()

    def arrived(ref, r_sem):
        pltpu.make_async_remote_copy(
            src_ref=ref, dst_ref=ref, send_sem=zs, recv_sem=r_sem,
            device_id=d_zp, device_id_type=MESH,
        ).wait_recv()

    def sent(ref, s_sem):
        pltpu.make_async_remote_copy(
            src_ref=ref, dst_ref=ref, send_sem=s_sem, recv_sem=wr.at[0],
            device_id=d_zp, device_id_type=MESH,
        ).wait_send()

    loads = [
        pltpu.make_async_copy(w, wbuf.at[i], w_sem.at[i])
        for i, w in enumerate((wk_hbm, wv_hbm, wq_hbm))
    ]
    for load in loads:
        load.start()
    own_out = pltpu.make_async_copy(
        wo_hbm.at[:, pl.ds(pl.multiple_of(hd * COLS, COLS), COLS)], wo.at[hd], w_sem.at[3]
    )
    own_out.start()

    barrier = pltpu.get_barrier_semaphore()
    peers = [d_xp, d_xm, d_yp, d_ym, d_zp, d_zm, d_core]
    peers += [wpeers[i][1] for i in (2, 4, 5, 6)]
    for peer in peers:
        pl.semaphore_signal(barrier, inc=1, device_id=peer, device_id_type=MESH)
    pl.semaphore_wait(barrier, len(peers))

    def x_arrived(at, r_sem):
        arrived(at((xm // 2) * 4 + y), r_sem.at[0])
        arrived(at((xp // 2) * 4 + y), r_sem.at[1])

    def y_first(at, s_sem, r_sem):
        send(at(y), at(y), s_sem, r_sem.at[0], d_yp)
        send(at(4 + y), at(4 + y), s_sem, r_sem.at[1], d_ym)
        send(at(4 + y), at(4 + y), s_sem, r_sem.at[2], d_yp)
        send(at(y), at(y), s_sem, r_sem.at[3], d_ym)

    def y_second(at, s_sem, r_sem):
        arrived(at(ym), r_sem.at[0])
        send(at(ym), at(ym), s_sem, r_sem.at[4], d_yp)
        arrived(at(4 + yp), r_sem.at[1])
        send(at(4 + yp), at(4 + yp), s_sem, r_sem.at[5], d_ym)
        arrived(at(4 + ym), r_sem.at[2])
        arrived(at(yp), r_sem.at[3])

    def y_last(at, r_sem):
        arrived(at(y2), r_sem.at[4])
        arrived(at(4 + y2), r_sem.at[5])

    def tok_at(r):
        return lambda g: tok.at[r, g]

    def att_at(h):
        return lambda g: att.at[h, g]

    def rows_of(g):
        return pl.ds(pl.multiple_of(g * COLS, COLS), COLS)

    def product(r, yy, h):
        left = jnp.concatenate([tok[r, yy], tok[r, 4 + yy]], axis=1)
        cols = pl.ds(pl.multiple_of(h * HD, HD), HD)
        right = jnp.concatenate(
            [
                jnp.concatenate([wbuf[i, rows_of(g), cols] for i in range(3)], axis=1)
                for g in (yy, 4 + yy)
            ],
            axis=0,
        )
        return jnp.dot(left, right, preferred_element_type=jnp.float32)

    def project(r, yy, first=False):
        def one(h, carry):
            part = product(r, yy, h)
            acc[r, h] = part if first else acc[r, h] + part
            return carry

        lax.fori_loop(0, HEADS, one, 0)

    def z_send(direction, s, h, r):
        if s == 4 and direction != r:
            return
        if direction == 0:
            ref, to = kv.at[(z + NZ - (s - 1)) % NZ, h, r], d_zp
        else:
            ref, to = kv.at[(z + (s - 1)) % NZ, h, r], d_zm
        send(ref, ref, zs, zr.at[direction, s - 1, h, r], to)

    def z_arrived(direction, s, h, r):
        if s == 4 and direction != r:
            return
        src = (z + NZ - s) % NZ if direction == 0 else (z + s) % NZ
        arrived(kv.at[src, h, r], zr.at[direction, s - 1, h, r])

    def z_start(h, r):
        z_send(0, 1, h, r)
        z_send(1, 1, h, r)

    def z_round(k):
        for s in (4, 3, 2, 1):
            for r in range(2):
                for h in range(HEADS):
                    if k == START[r][h] + s:
                        for direction in range(2):
                            z_arrived(direction, s, h, r)
                            if s < 4:
                                z_send(direction, s + 1, h, r)
        for h in range(HEADS):
            if k == START[1][h] and k > START[1][0]:
                z_start(h, 1)

    me_slot, core_slot = x_lo * 2 + c, x_lo * 2 + pc
    far_slot, far_core_slot = x_far * 2 + c, x_far * 2 + pc

    def finish(r):
        for h in range(HEADS):
            rows = acc[r, h] + product(r, y2, h)
            kv[z, h, r, 0] = rows[:, 0:HD].astype(jnp.bfloat16)
            kv[z, h, r, 1] = jnp.transpose(rows[:, HD : 2 * HD]).astype(jnp.bfloat16)
            qall[me_slot, r, h] = rows[:, 2 * HD :].astype(jnp.bfloat16)
            if START[r][h] == START[r][0]:
                z_start(h, r)
        mine = qall.at[me_slot, r]
        send(mine, mine, qs, qr.at[r, 0], d_far)
        send(mine, mine, qs, qr.at[r, 1], d_core)

    def q_relay(r):
        theirs = qall.at[far_slot, r]
        arrived(theirs, qr.at[r, 0])
        send(theirs, theirs, qs, qr.at[r, 2], d_core)

    def q_arrived():
        for r in range(2):
            arrived(qall.at[core_slot, r], qr.at[r, 1])
            arrived(qall.at[far_core_slot, r], qr.at[r, 2])

    half = COLS // 2
    my_half = pl.ds(pl.multiple_of(c * half, half), half)
    other_half = pl.ds(pl.multiple_of(pc * half, half), half)

    def out_weights():
        for i, (g, to) in enumerate(wpeers):
            send(
                wo_hbm.at[my_half, pl.ds(pl.multiple_of(g * COLS, COLS), COLS)],
                wo.at[hd, my_half, :], ws, wr.at[i], to,
            )

    def out_weights_relay():
        for i, j in enumerate((1, 0, 2, 3, 5, 4, 6)):
            piece = wo.at[wpeers[i][0], my_half, :]
            arrived(piece, wr.at[j])
            send(piece, piece, ws, wr.at[7 + i], d_core)

    def out_weights_arrived():
        own_out.wait()
        for i in range(7):
            arrived(wo.at[wpeers[i][0], other_half, :], wr.at[7 + i])

    def bias_row(q_slot, src, r):
        q_ctx = (1 - q_slot // 2) * 16 + z * 2 + q_slot % 2
        k_ctx = x_far * 16 + src * 2 + c
        key_block = order_ref[2 * k_ctx + r]
        parts = []
        for qi in range(2):
            live = mask_ref[order_ref[2 * q_ctx + qi], key_block]
            bias = jnp.where(live > 0, 0.0, NEG).astype(jnp.float32)
            parts.append(jnp.full((1, BLK), bias, jnp.float32))
        return jnp.concatenate(parts, axis=1)

    def attend(h, r, group):
        first = r == 0 and group == 0
        srcs = [(z + NZ + sign * dist) % NZ for dist, sign in GROUPS[group]]

        def body(slot, carry):
            q = jnp.concatenate([qall[slot, 0, h], qall[slot, 1, h]], axis=0)
            keys = jnp.concatenate([kv[src, h, r, 0] for src in srcs], axis=0)
            raw = lax.dot_general(
                keys, q, (((1,), (1,)), ((), ())), preferred_element_type=jnp.float32
            )
            blocks = [raw[i * BLK : (i + 1) * BLK] for i in range(len(srcs))]
            biases = [bias_row(slot, src, r) for src in srcs]
            tops = [
                jnp.max(b.reshape(BLK // 8, 8, ROWS), axis=0) * SCALE2 + bias
                for b, bias in zip(blocks, biases)
            ]
            top = jnp.max(functools.reduce(jnp.maximum, tops), axis=0, keepdims=True)
            before = jnp.full((1, ROWS), LOW, jnp.float32) if first else m_s[h, slot, 0:1]
            top = jnp.maximum(before, top)
            weights = [
                jnp.exp2(b * SCALE2 - (top - bias)) for b, bias in zip(blocks, biases)
            ]
            total = functools.reduce(
                jnp.add, [jnp.sum(w.reshape(BLK // 8, 8, ROWS), axis=0) for w in weights]
            )
            rounded = jnp.concatenate([w.astype(jnp.bfloat16) for w in weights], axis=0)
            values = jnp.concatenate([kv[src, h, r, 1] for src in srcs], axis=1)
            mixed = jnp.dot(values, rounded, preferred_element_type=jnp.float32)
            if not first:
                factor = jnp.exp2(before - top)
                total = total + l_s[h, slot] * factor
                mixed = mixed + o_s[h, slot] * factor
            m_s[h, slot, 0:1] = top
            l_s[h, slot] = total
            o_s[h, slot] = mixed
            return carry

        lax.fori_loop(0, 4, body, 0, unroll=1)

    def stats(h, slot):
        return m_s[h, slot, 0:1], jnp.sum(l_s[h, slot], axis=0, keepdims=True), o_s[h, slot]

    def merge(a, b):
        top = jnp.maximum(a[0], b[0])
        fa, fb = jnp.exp2(a[0] - top), jnp.exp2(b[0] - top)
        return top, a[1] * fa + b[1] * fb, a[2] * fa + b[2].astype(jnp.float32) * fb

    def share(h):
        for i, slot in enumerate((core_slot, far_core_slot)):
            top, total, mixed = stats(h, slot)
            s1[h, i, 0:1] = top
            s1[h, i, 1:2] = total
            o1[h, i] = mixed.astype(jnp.bfloat16)
        send(s1.at[h], s1r.at[h], cs.at[0], cr.at[h, 0], d_core)
        send(o1.at[h], o1r.at[h], cs.at[1], cr.at[h, 1], d_core)

    def mid(h):
        arrived(s1r.at[h], cr.at[h, 0])
        arrived(o1r.at[h], cr.at[h, 1])
        top, total, mixed = merge(
            stats(h, far_slot), (s1r[h, 1, 0:1], s1r[h, 1, 1:2], o1r[h, 1])
        )
        s2[h, 0:1] = top
        s2[h, 1:2] = total
        o2[h] = mixed.astype(jnp.bfloat16)
        send(s2.at[h], s2r.at[h], cs.at[2], cr.at[h, 2], d_far)
        send(o2.at[h], o2r.at[h], cs.at[3], cr.at[h, 3], d_far)
        top, total, mixed = merge(
            stats(h, me_slot), (s1r[h, 0, 0:1], s1r[h, 0, 1:2], o1r[h, 0])
        )
        m_s[h, me_slot, 0:1] = top
        m_s[h, me_slot, 1:2] = total
        o_s[h, me_slot] = mixed

    def fin(h):
        arrived(s2r.at[h], cr.at[h, 2])
        arrived(o2r.at[h], cr.at[h, 3])
        _, total, mixed = merge(
            (m_s[h, me_slot, 0:1], m_s[h, me_slot, 1:2], o_s[h, me_slot]),
            (s2r[h, 0:1], s2r[h, 1:2], o2r[h]),
        )
        asend[h] = jnp.transpose(mixed / total).astype(jnp.bfloat16)
        send(asend.at[h], att.at[h, hd], as_, axr.at[h, 0], d_xp)
        send(asend.at[h], att.at[h, hd], as_, axr.at[h, 1], d_xm)

    def g1(h):
        x_arrived(att_at(h), axr.at[h])
        y_first(att_at(h), as_, ayr.at[h])

    def g2(h):
        y_second(att_at(h), as_, ayr.at[h])

    def out_part(h, yy, first=False):
        rows = slice(h * HD, (h + 1) * HD)
        left = jnp.concatenate([att[h, yy], att[h, 4 + yy]], axis=1)
        right = jnp.concatenate([wo[yy, rows, :], wo[4 + yy, rows, :]], axis=0)
        part = jnp.dot(left, right, preferred_element_type=jnp.float32)
        out_acc[...] = part if first else out_acc[...] + part

    def g3(h):
        out_part(h, y, h == 0)
        out_part(h, ym)
        out_part(h, yp)
        y_last(att_at(h), ayr.at[h])
        out_part(h, y2)

    for r in range(2):
        src = tok_in.at[pl.ds(r * HALF, HALF), :]
        send(src, tok.at[r, hd], xs, xr.at[r, 0], d_xp)
        send(src, tok.at[r, hd], xs, xr.at[r, 1], d_xm)
    x_arrived(tok_at(0), xr.at[0])
    y_first(tok_at(0), ys, yr.at[0])
    for load in loads:
        load.wait()
    project(0, y, True)
    y_second(tok_at(0), ys, yr.at[0])
    x_arrived(tok_at(1), xr.at[1])
    y_first(tok_at(1), ys, yr.at[1])
    project(0, ym)
    project(0, yp)
    y_last(tok_at(0), yr.at[0])
    finish(0)
    project(1, y, True)
    y_second(tok_at(1), ys, yr.at[1])
    z_round(1)
    project(1, ym)
    project(1, yp)
    y_last(tok_at(1), yr.at[1])
    z_round(2)
    finish(1)
    out_weights()
    q_relay(0)
    z_round(3)
    q_relay(1)
    q_arrived()
    attend(0, 0, 0)
    attend(1, 0, 0)
    z_round(4)
    attend(2, 0, 0)
    attend(0, 0, 1)
    z_round(5)
    attend(1, 0, 1)
    attend(2, 0, 1)
    attend(0, 1, 0)
    z_round(6)
    attend(0, 1, 1)
    share(0)
    attend(1, 1, 0)
    z_round(7)
    mid(0)
    attend(1, 1, 1)
    share(1)
    z_round(8)
    out_weights_relay()
    attend(2, 1, 0)
    mid(1)
    fin(0)
    attend(2, 1, 1)
    share(2)
    out_weights_arrived()
    mid(2)
    fin(1)
    g1(0)
    fin(2)
    g1(1)
    g2(0)
    g1(2)
    g2(1)
    g3(0)
    g2(2)
    g3(1)
    g3(2)
    out_ref[...] = out_acc[...].astype(jnp.bfloat16)

    sent(tok.at[0, 0:4], xs)
    sent(tok.at[:, 0:6], ys)
    sent(kv.at[0:7], zs)
    sent(tok.at[0, 0:6], qs)
    sent(s1, cs.at[0])
    sent(o1, cs.at[1])
    sent(s2, cs.at[2])
    sent(o2, cs.at[3])
    sent(att, as_)
    sent(wo.at[0:7], ws)


def per_device(tokens, block_order, block_mask, w_query, w_key, w_value, w_out):
    bf, f32 = jnp.bfloat16, jnp.float32
    sem = pltpu.SemaphoreType.DMA
    smem = pl.BlockSpec(memory_space=pltpu.SMEM)
    vmem = pl.BlockSpec(memory_space=pltpu.VMEM)
    anywhere = pl.BlockSpec(memory_space=pl.ANY)
    return pl.pallas_call(
        kernel,
        out_shape=jax.ShapeDtypeStruct((ROWS, COLS), bf),
        in_specs=[smem, smem, vmem, anywhere, anywhere, anywhere, anywhere],
        out_specs=vmem,
        scratch_shapes=[
            pltpu.VMEM((2, 8, HALF, COLS), bf),
            pltpu.VMEM((3, 3072, COLS), bf),
            pltpu.VMEM((8, COLS, COLS), bf),
            pltpu.VMEM((2, HEADS, HALF, 3 * HD), f32),
            pltpu.VMEM((4, 2, HEADS, HALF, HD), bf),
            pltpu.VMEM((NZ, HEADS, 2, 2, HALF, HD), bf),
            pltpu.VMEM((HEADS, 4, 8, ROWS), f32),
            pltpu.VMEM((HEADS, 4, 8, ROWS), f32),
            pltpu.VMEM((HEADS, 4, HD, ROWS), f32),
            pltpu.VMEM((HEADS, 2, HD, ROWS), bf),
            pltpu.VMEM((HEADS, 2, 8, ROWS), f32),
            pltpu.VMEM((HEADS, 2, HD, ROWS), bf),
            pltpu.VMEM((HEADS, 2, 8, ROWS), f32),
            pltpu.VMEM((HEADS, HD, ROWS), bf),
            pltpu.VMEM((HEADS, 8, ROWS), f32),
            pltpu.VMEM((HEADS, HD, ROWS), bf),
            pltpu.VMEM((HEADS, 8, ROWS), f32),
            pltpu.VMEM((HEADS, ROWS, HD), bf),
            pltpu.VMEM((HEADS, 8, ROWS, HD), bf),
            pltpu.VMEM((ROWS, COLS), f32),
            sem((4,)),
            sem, sem((2, 2)),
            sem, sem((2, 6)),
            sem, sem((2, 4, HEADS, 2)),
            sem, sem((2, 3)),
            sem((4,)), sem((HEADS, 4)),
            sem, sem((HEADS, 2)), sem((HEADS, 6)),
            sem, sem((14,)),
        ],
        compiler_params=pltpu.CompilerParams(
            collective_id=0, has_side_effects=True, vmem_limit_bytes=60 * 1024 * 1024
        ),
    )(block_order, block_mask, tokens, w_query, w_key, w_value, w_out)


def solution(mesh):
    in_specs = (
        P("ctx", "head"),
        P(),
        P(),
        P(None, "head"),
        P(None, "head"),
        P(None, "head"),
        P("head", None),
    )
    return jax.shard_map(
        per_device, mesh=mesh, in_specs=in_specs, out_specs=P("ctx", "head"), check_vma=False
    )
```
